32 devices in a mesh: ty: 4 (over x, core), tx: 8 (over z, y).
Axes of the slice: x: 2, y: 2, z: 4, core: 2. Of those that a mesh axis runs over, the one named last changes fastest.
Arguments:
- intensity: float32 [64, 256, 256], P(('ty', 'tx')), may hold values from 0 to 3
- corner: int32 [64, 2], P(('ty', 'tx')), may hold values from 0 to 768, as said below
- probe: float32 [2, 256, 256], replicated, may hold values from -6 to 6
- prop_phase: float32 [256, 256], replicated, may hold values from -3.140625 to 3.140625
- object_slices: float32 [2, 2, 1024, 1024], P(None, None, 'ty', 'tx'), may hold values from -5 to 5
- momentum: float32 [2, 2, 1024, 1024], P(None, None, 'ty', 'tx'), may hold values from -6 to 6
Outputs:
- object_next: float32 [2, 2, 1024, 1024], P(None, None, 'ty', 'tx')
- momentum_next: float32 [2, 2, 1024, 1024], P(None, None, 'ty', 'tx')
The draws below stay inside these ranges and needn't reach their ends.
Inputs may be any that keep to these rules, and one draw needn't show every extreme that they name: `corner`: patch p belongs to device p // 2 of ty+tx (ty slowest); with t = p // (2 times the size of tx) and s = (p // 2) modulo the size of tx, its row offset lies between max(t * 256 - 256 / 2, 0) and min(t * 256 + 256 - 256 / 2, 768), and its column offset between max(s * 128 - 256 / 2, 0) and min(s * 128 + 128 - 256 / 2, 768).
All inputs are finite; a program needn't handle non-finite values.
Results may differ from the reference program's by a relative error of at most 0.0003.
Values sent between devices are 32-bit elements; how exact they have to be, the bound alone decides.
A program may use at most 64 MiB of HBM per device.

```python
import jax
import jax.numpy as jnp
from jax import lax

PATCH = 256
PAT_DEV = 2
TILE_Y = 256
TILE_X = 128
PATCHES = 64
OY = 1024
OX = 1024
N_TX = 8


def draw_corner(key, part):
    member = jnp.arange(PATCHES, dtype=jnp.int32)
    tile_row = member // (PAT_DEV * N_TX)
    tile_col = member // PAT_DEV % N_TX
    row_low = jnp.maximum(tile_row * TILE_Y - PATCH // 2, 0)
    row_high = jnp.minimum(tile_row * TILE_Y + TILE_Y - PATCH // 2, OY - PATCH)
    col_low = jnp.maximum(tile_col * TILE_X - PATCH // 2, 0)
    col_high = jnp.minimum(tile_col * TILE_X + TILE_X - PATCH // 2, OX - PATCH)
    row_key, col_key = jax.random.split(jax.random.fold_in(key, 7))
    row_start = jax.random.randint(row_key, (PATCHES,), row_low, row_high + 1)
    col_start = jax.random.randint(col_key, (PATCHES,), col_low, col_high + 1)
    return jnp.stack([row_start, col_start], axis=1).astype(jnp.int32)


def level_of(own_key, extent, cuts, smallest, top_value):
    def one(dim, blocks):
        steps = jax.random.uniform(jax.random.fold_in(jax.random.fold_in(own_key, 6), dim), (blocks,), jnp.float32, smallest / len(cuts), top_value / len(cuts))
        return jnp.repeat(jnp.exp(steps), extent[dim] // blocks).reshape((-1,) + (1,) * (len(extent) - dim - 1))

    level = one(*cuts[0])
    for cut in cuts[1:]:
        level = level * one(*cut)
    return level


def normal_values(key, extent, deviation, bound, cuts=(), kind=jnp.bfloat16):
    result = deviation * jax.random.normal(key, extent, jnp.float32)
    if cuts:
        result = result * level_of(key, extent, cuts, -0.22, 0.18)
    return jnp.clip(result, -bound, bound).astype(kind)


def setup_inputs(seed: int = 0) -> dict:
    streams_of = jax.random.split(jax.random.key(seed), 7)
    intensity = jnp.clip(3.0 * jax.random.uniform(streams_of[0], (PATCHES, PATCH, PATCH), jnp.float32) ** level_of(streams_of[0], (PATCHES, PATCH, PATCH), ((0, 32),), -0.2, 0.2), 0.0, 3.0)
    corner = draw_corner(jax.random.fold_in(streams_of[6], 71), 0)
    probe = normal_values(streams_of[2], (2, PATCH, PATCH), 1.0, 6.0, (), jnp.float32)
    prop_phase = jnp.clip(jax.random.uniform(streams_of[3], (PATCH, PATCH), jnp.float32, -3.140625, 3.140625), -3.140625, 3.140625)
    object_slices = normal_values(streams_of[4], (2, 2, OY, OX), 0.7, 5.0, ((2, 4), (3, 8)), jnp.float32)
    momentum = normal_values(streams_of[5], (2, 2, OY, OX), 1.0, 6.0, ((2, 4), (3, 8)), jnp.float32)
    return dict(intensity=intensity, corner=corner, probe=probe, prop_phase=prop_phase, object_slices=object_slices, momentum=momentum)


decay_rate = 0.9
grad_scale = 0.05
step_length = 0.5


def forward(field):
    return jnp.fft.fft2(field, norm="ortho")


def inverse(field):
    return jnp.fft.ifft2(field, norm="ortho")


def reference(intensity, corner, probe, prop_phase, object_slices, momentum):
    probe_wave = lax.complex(probe[0], probe[1])
    transfer = lax.complex(jnp.cos(prop_phase), jnp.sin(prop_phase))
    objects = lax.complex(object_slices[:, 0], object_slices[:, 1])

    def accumulate(gradient, packed):
        offsets, measured = packed
        start = (jnp.zeros((), jnp.int32), offsets[0].astype(jnp.int32), offsets[1].astype(jnp.int32))
        window = lax.dynamic_slice(objects, start, (2, PATCH, PATCH))
        exit_wave = inverse(transfer * forward(probe_wave * window[0]))
        far_field = forward(exit_wave * window[1])
        residue = far_field.real ** 2 + far_field.imag ** 2 - measured
        back_wave = inverse(2.0 * residue * far_field)
        second = jnp.conj(exit_wave) * back_wave
        first = jnp.conj(probe_wave) * inverse(jnp.conj(transfer) * forward(jnp.conj(window[1]) * back_wave))
        current = lax.dynamic_slice(gradient, start, (2, PATCH, PATCH))
        return lax.dynamic_update_slice(gradient, current + jnp.stack([first, second]), start), None

    gradient, unused = lax.scan(accumulate, jnp.zeros_like(objects), (corner, intensity))
    grad_parts = jnp.stack([gradient.real, gradient.imag], axis=1)
    momentum_next = decay_rate * momentum + grad_scale * grad_parts
    object_next = object_slices - step_length * momentum_next
    return object_next, momentum_next
```

```python
import functools
import math

import jax
import jax.numpy as jnp
import numpy as np
from jax import lax
from jax.experimental import pallas as pl
from jax.experimental.pallas import tpu as pltpu
from jax.sharding import PartitionSpec as P

decay_rate = 0.9
grad_scale = 0.05
step_length = 0.5

VMEM = pl.BlockSpec(memory_space=pltpu.VMEM)
SMEM = pl.BlockSpec(memory_space=pltpu.SMEM)


def dft_tables(n):
    k = np.arange(n)
    angle = 2.0 * math.pi * (np.outer(k, k) % n) / n
    c, s = np.cos(angle) / math.sqrt(n), -np.sin(angle) / math.sqrt(n)
    right = np.block([[c, s], [-s, c]]).astype(np.float32)
    left = np.concatenate([c, s], axis=0).astype(np.float32)

    def split(t):
        hi = t.astype(jnp.bfloat16)
        lo = (t - hi.astype(np.float32)).astype(jnp.bfloat16)
        return hi, lo

    rh, rl = split(right)
    lh, ll = split(left)
    return (
        jnp.asarray(np.concatenate([rh, rh, rl], axis=0)),
        jnp.asarray(np.concatenate([lh, lh, ll], axis=1)),
    )


def halves(x):
    hi = x.astype(jnp.bfloat16)
    lo = (x - hi.astype(jnp.float32)).astype(jnp.bfloat16)
    return hi, lo


def fft2(xr, xi, right_ref, left_ref):
    n = xr.shape[-1]
    hi, lo = halves(jnp.concatenate([xr, xi], axis=1))
    y = jnp.dot(
        jnp.concatenate([hi, lo, hi], axis=1), right_ref[...], preferred_element_type=jnp.float32
    )
    hi, lo = halves(y)
    z = jnp.dot(
        left_ref[...], jnp.concatenate([hi, lo, hi], axis=0), preferred_element_type=jnp.float32
    )
    return z[:n, :n] - z[n:, n:], z[:n, n:] + z[n:, :n]


def ifft2(xr, xi, right_ref, left_ref):
    yi, yr = fft2(xi, xr, right_ref, left_ref)
    return yr, yi


def mul(ar, ai, br, bi):
    return ar * br - ai * bi, ar * bi + ai * br


def masks(sc_ref, p, n):
    r, c, odd = sc_ref[p, 0], sc_ref[p, 1], sc_ref[p, 2]
    h = n // 2
    rows = lax.broadcasted_iota(jnp.int32, (n, h), 0)
    cols = lax.broadcasted_iota(jnp.int32, (n, h), 1)
    later = (cols >= c).astype(jnp.int32)
    return rows >= r, (later + odd) == 1


def window(q, p, sc_ref, tiles, above_ref, below_ref, n):
    h = n // 2
    row_first, use_far = masks(sc_ref, p, n)
    cols = []
    for t, tile in enumerate(tiles):
        top = jnp.where(row_first[:h], above_ref[t, q], tile[q, h:, :])
        bottom = jnp.where(row_first[h:], tile[q, :h, :], below_ref[t, q])
        cols.append(jnp.concatenate([top, bottom], axis=0))
    own, partner, far = cols
    return jnp.concatenate([jnp.where(use_far, far, partner), own], axis=1)


def scatter(g, q, p, sc_ref, tiles, above_ref, below_ref, n):
    h = n // 2
    row_first, use_far = masks(sc_ref, p, n)
    left, own = g[:, :h], g[:, h:]
    zero = jnp.zeros_like(left)
    parts = (own, jnp.where(use_far, zero, left), jnp.where(use_far, left, zero))
    for t, (tile, v) in enumerate(zip(tiles, parts)):
        low = jnp.where(row_first, v, zero)
        high = jnp.where(row_first, zero, v)
        above_ref[t, q] += low[:h]
        tile[q, h:, :] += high[:h]
        tile[q, :h, :] += low[h:]
        below_ref[t, q] += high[h:]


def first_kernel(sc_ref, probe_ref, tr_ref, right_ref, left_ref, own, partner, far, above_ref, below_ref, phi_ref, roll_ref):
    n = probe_ref.shape[-1]

    def body(p, carry):
        r, c = lax.rem(sc_ref[p, 0], n), sc_ref[p, 1]
        pr = pltpu.roll(pltpu.roll(probe_ref[0], c, 1), r, 0)
        pi = pltpu.roll(pltpu.roll(probe_ref[1], c, 1), r, 0)
        roll_ref[p, 0] = pr
        roll_ref[p, 1] = pi
        tiles = (own, partner, far)
        wr = window(0, p, sc_ref, tiles, above_ref, below_ref, n)
        wi = window(1, p, sc_ref, tiles, above_ref, below_ref, n)
        xr, xi = fft2(*mul(pr, pi, wr, wi), right_ref, left_ref)
        xr, xi = ifft2(*mul(tr_ref[0], tr_ref[1], xr, xi), right_ref, left_ref)
        phi_ref[p, 0] = xr
        phi_ref[p, 1] = xi
        return carry

    lax.fori_loop(0, phi_ref.shape[0], body, 0)


def clear(refs):
    for ref in refs:
        ref[...] = jnp.zeros_like(ref)


def second_kernel(sc_ref, phi_ref, intensity_ref, right_ref, left_ref, own, partner, far, above_ref, below_ref, back_ref, g_own, g_partner, g_far, g_above, g_below):
    n = intensity_ref.shape[-1]
    clear((g_own, g_partner, g_far, g_above, g_below))

    def body(p, carry):
        tiles = (own, partner, far)
        wr = window(0, p, sc_ref, tiles, above_ref, below_ref, n)
        wi = window(1, p, sc_ref, tiles, above_ref, below_ref, n)
        pr, pi = phi_ref[p, 0], phi_ref[p, 1]
        fr, fi = fft2(*mul(pr, pi, wr, wi), right_ref, left_ref)
        res = 2.0 * (fr * fr + fi * fi - intensity_ref[p])
        br, bi = ifft2(res * fr, res * fi, right_ref, left_ref)
        zr, zi = mul(wr, -wi, br, bi)
        back_ref[p, 0] = zr
        back_ref[p, 1] = zi
        gr, gi = mul(phi_ref[p, 0], -phi_ref[p, 1], br, bi)
        outs = (g_own, g_partner, g_far)
        scatter(gr, 0, p, sc_ref, outs, g_above, g_below, n)
        scatter(gi, 1, p, sc_ref, outs, g_above, g_below, n)
        return carry

    lax.fori_loop(0, phi_ref.shape[0], body, 0)


def third_kernel(sc_ref, back_ref, roll_ref, tr_ref, right_ref, left_ref, g_own, g_partner, g_far, g_above, g_below):
    n = back_ref.shape[-1]
    clear((g_own, g_partner, g_far, g_above, g_below))

    def body(p, carry):
        xr, xi = fft2(back_ref[p, 0], back_ref[p, 1], right_ref, left_ref)
        xr, xi = ifft2(*mul(tr_ref[0], -tr_ref[1], xr, xi), right_ref, left_ref)
        gr, gi = mul(roll_ref[p, 0], -roll_ref[p, 1], xr, xi)
        outs = (g_own, g_partner, g_far)
        scatter(gr, 0, p, sc_ref, outs, g_above, g_below, n)
        scatter(gi, 1, p, sc_ref, outs, g_above, g_below, n)
        return carry

    lax.fori_loop(0, back_ref.shape[0], body, 0)


def call(kernel, outs, args, flops):
    return pl.pallas_call(
        kernel,
        out_shape=[jax.ShapeDtypeStruct(s, jnp.float32) for s in outs],
        in_specs=[SMEM] + [VMEM] * (len(args) - 1),
        out_specs=[VMEM] * len(outs),
        compiler_params=pltpu.CompilerParams(vmem_limit_bytes=48 << 20),
        cost_estimate=pl.CostEstimate(flops=flops, bytes_accessed=8 << 20, transcendentals=0),
    )(*args)


def on_device(intensity, corner, probe, prop_phase, object_slices, momentum):
    count, n = intensity.shape[0], intensity.shape[-1]
    h = n // 2
    _, _, tile_rows, tile_cols = object_slices.shape
    assert tile_rows == n and tile_cols == h
    nty, ntx = lax.axis_size("ty"), lax.axis_size("tx")
    assert ntx % 2 == 0
    iy, ix = lax.axis_index("ty"), lax.axis_index("tx")
    odd = ix % 2
    sc = jnp.stack(
        [
            corner[:, 0] - (iy * tile_rows - h),
            corner[:, 1] - (ix * tile_cols - h),
            jnp.full((count,), odd, jnp.int32),
        ],
        axis=1,
    )
    swap = [(i, i ^ 1) for i in range(ntx)]
    even_up = [(i, i + 2) for i in range(0, ntx - 2, 2)]
    odd_down = [(i + 2, i) for i in range(1, ntx - 2, 2)]
    relay = even_up + odd_down
    back = [(j, i) for i, j in relay]
    down = [(i, i + 1) for i in range(nty - 1)]
    up = [(i + 1, i) for i in range(nty - 1)]

    def halo(s):
        own = object_slices[s]
        partner = lax.ppermute(own, "tx", swap)
        far = lax.ppermute(partner, "tx", relay)
        above = lax.ppermute(jnp.stack([t[:, h:] for t in (own, partner, far)]), "ty", down)
        below = lax.ppermute(jnp.stack([t[:, :h] for t in (own, partner, far)]), "ty", up)
        return own, partner, far, above, below

    def fold(own, partner, far, above, below):
        from_below = lax.ppermute(above, "ty", up)
        from_above = lax.ppermute(below, "ty", down)

        def rows(tile, t):
            return tile + jnp.concatenate([from_above[t], from_below[t]], axis=1)

        far_in = lax.ppermute(rows(far, 2), "tx", back)
        partner_in = lax.ppermute(rows(partner, 1) + far_in, "tx", swap)
        return rows(own, 0) + partner_in

    right, left = dft_tables(n)
    transfer = jnp.stack([jnp.cos(prop_phase), jnp.sin(prop_phase)])
    field = (count, 2, n, n)
    bands = [(2, n, h)] * 3 + [(3, 2, h, h)] * 2
    flops = 2 * 48 * count * n * n * n
    halo_first = halo(0)
    halo_second = halo(1)
    phi, rolled = call(first_kernel, [field, field], (sc, probe, transfer, right, left) + halo_first, flops)
    back_wave, *bands_second = call(
        second_kernel, [field] + bands, (sc, phi, intensity, right, left) + halo_second, flops
    )
    bands_first = call(third_kernel, bands, (sc, back_wave, rolled, transfer, right, left), flops)
    grad_second = fold(*bands_second)
    grad_first = fold(*bands_first)
    gradient = jnp.stack([grad_first, grad_second])
    momentum_next = decay_rate * momentum + grad_scale * gradient
    object_next = object_slices - step_length * momentum_next
    return (object_next, momentum_next)


def solution(mesh):
    return jax.shard_map(
        on_device,
        mesh=mesh,
        in_specs=(
            P(("ty", "tx"), None, None),
            P(("ty", "tx"), None),
            P(),
            P(),
            P(None, None, "ty", "tx"),
            P(None, None, "ty", "tx"),
        ),
        out_specs=(P(None, None, "ty", "tx"), P(None, None, "ty", "tx")),
        check_vma=False,
    )
```

```python
import functools
import math

import jax
import jax.numpy as jnp
import numpy as np
from jax import lax
from jax.experimental import pallas as pl
from jax.experimental.pallas import tpu as pltpu
from jax.sharding import PartitionSpec as P

decay_rate = 0.9
grad_scale = 0.05
step_length = 0.5

VMEM = pl.BlockSpec(memory_space=pltpu.VMEM)
ANY = pl.BlockSpec(memory_space=pl.ANY)
SMEM = pl.BlockSpec(memory_space=pltpu.SMEM)


def dft_tables(n):
    k = np.arange(n)
    angle = 2.0 * math.pi * (np.outer(k, k) % n) / n
    c, s = np.cos(angle) / math.sqrt(n), -np.sin(angle) / math.sqrt(n)
    right = np.block([[c, s], [-s, c]]).astype(np.float32)
    left = np.concatenate([c, s], axis=0).astype(np.float32)

    def split(t):
        hi = t.astype(jnp.bfloat16)
        lo = (t - hi.astype(np.float32)).astype(jnp.bfloat16)
        return hi, lo

    rh, rl = split(right)
    lh, ll = split(left)
    return (
        jnp.asarray(np.concatenate([rh, rh, rl], axis=0)),
        jnp.asarray(np.concatenate([lh, lh, ll], axis=1)),
    )


def halves(x):
    hi = x.astype(jnp.bfloat16)
    lo = (x - hi.astype(jnp.float32)).astype(jnp.bfloat16)
    return hi, lo


def fft2(xr, xi, right_ref, left_ref):
    n = xr.shape[-1]
    hi, lo = halves(jnp.concatenate([xr, xi], axis=1))
    y = jnp.dot(
        jnp.concatenate([hi, lo, hi], axis=1), right_ref[...], preferred_element_type=jnp.float32
    )
    hi, lo = halves(y)
    z = jnp.dot(
        left_ref[...], jnp.concatenate([hi, lo, hi], axis=0), preferred_element_type=jnp.float32
    )
    return z[:n, :n] - z[n:, n:], z[:n, n:] + z[n:, :n]


def ifft2(xr, xi, right_ref, left_ref):
    yi, yr = fft2(xi, xr, right_ref, left_ref)
    return yr, yi


def mul(ar, ai, br, bi):
    return ar * br - ai * bi, ar * bi + ai * br


def masks(sc_ref, p, n, odd):
    r, c = sc_ref[p, 0], sc_ref[p, 1]
    h = n // 2
    rows = lax.broadcasted_iota(jnp.int32, (n, h), 0)
    cols = lax.broadcasted_iota(jnp.int32, (n, h), 1)
    later = (cols >= c).astype(jnp.int32)
    return rows >= r, (later + odd) == 1


def window(q, tiles, edge, mask, n):
    h = n // 2
    row_first, use_far = mask
    cols = []
    for t, tile in enumerate(tiles):
        top = jnp.where(row_first[:h], edge[1, t, q], tile[q, h:, :])
        bottom = jnp.where(row_first[h:], tile[q, :h, :], edge[0, t, q])
        cols.append(jnp.concatenate([top, bottom], axis=0))
    own, partner, far = cols
    return jnp.concatenate([jnp.where(use_far, far, partner), own], axis=1)


def scatter(g, q, g_tile, g_edge, mask, n):
    h = n // 2
    row_first, use_far = mask
    left, own = g[:, :h], g[:, h:]
    zero = jnp.zeros_like(left)
    parts = (own, jnp.where(use_far, zero, left), jnp.where(use_far, left, zero))
    for t, v in enumerate(parts):
        low = jnp.where(row_first, v, zero)
        high = jnp.where(row_first, zero, v)
        g_edge[1, t, q] += low[:h]
        g_tile[t, q, h:, :] += high[:h]
        g_tile[t, q, :h, :] += low[h:]
        g_edge[0, t, q] += high[h:]


def kernel(
    sizes, sc_ref, own, probe_ref, phase_ref, intensity_hbm, right_hbm, left_hbm, out_ref,
    right_ref, left_ref, intensity_ref, tr_ref, roll_ref, phi_ref, back_ref,
    part, far, edge, g_tile, g_edge, rows_in, far_in, part_in,
    local_sem, m_send, m_recv, f_send, f_recv, e_send, e_recv,
    r_send, r_recv, gf_send, gf_recv, gp_send, gp_recv,
):
    nty, ntx = sizes
    count, n = intensity_ref.shape[0], intensity_ref.shape[-1]
    h = n // 2
    iy, ix = lax.axis_index("ty"), lax.axis_index("tx")
    odd = lax.rem(ix, 2)
    partner = ix + 1 - 2 * odd
    target = ix + 2 - 4 * odd
    source = ix - 2 + 4 * odd
    has_target = jnp.logical_and(target >= 0, target < ntx)
    has_source = jnp.logical_and(source >= 0, source < ntx)
    has_up, has_down = iy > 0, iy < nty - 1
    vertical = ((iy - 1, has_up), (iy + 1, has_down))

    loads = [
        pltpu.make_async_copy(a, b, local_sem.at[i])
        for i, (a, b) in enumerate(
            ((right_hbm, right_ref), (left_hbm, left_ref), (intensity_hbm, intensity_ref))
        )
    ]
    for load in loads:
        load.start()

    barrier = pltpu.get_barrier_semaphore()

    def greet(dev):
        pl.semaphore_signal(barrier, inc=1, device_id=dev, device_id_type=pl.DeviceIdType.MESH)

    greet((iy, partner))
    for cond, dev in (
        (has_target, (iy, target)),
        (has_source, (iy, source)),
        (has_up, (iy - 1, ix)),
        (has_down, (iy + 1, ix)),
    ):
        pl.when(cond)(functools.partial(greet, dev))
    peers = 1 + sum(cond.astype(jnp.int32) for cond in (has_target, has_source, has_up, has_down))
    pl.semaphore_wait(barrier, peers)

    def remote(src, dst, send, recv, dev):
        return pltpu.make_async_remote_copy(
            src_ref=src, dst_ref=dst, send_sem=send, recv_sem=recv,
            device_id=dev, device_id_type=pl.DeviceIdType.MESH,
        )

    def half(b):
        return pl.ds(b * h, h)

    def swap_copy(s, q, b):
        return remote(own.at[s, q, half(b)], part.at[s, q, half(b)], m_send.at[s, q, b], m_recv.at[s, q, b], (iy, partner))

    def relay_copy(s, q, b):
        return remote(part.at[s, q, half(b)], far.at[s, q, half(b)], f_send.at[s, q, b], f_recv.at[s, q, b], (iy, target))

    def edge_copy(s, q, b, t):
        src = (own, part, far)[t]
        return remote(src.at[s, q, half(b)], edge.at[s, b, t, q], e_send.at[s, b, t, q], e_recv.at[s, b, t, q], (vertical[b][0], ix))

    def rows_copy(s, q, b, t):
        return remote(g_edge.at[s, b, t, q], rows_in.at[s, b, t, q], r_send.at[s, b, t, q], r_recv.at[s, b, t, q], (vertical[1 - b][0], ix))

    def far_copy(s, q, b):
        return remote(g_tile.at[s, 2, q, half(b)], far_in.at[s, q, half(b)], gf_send.at[s, q, b], gf_recv.at[s, q, b], (iy, source))

    def part_copy(s, q, b):
        return remote(g_tile.at[s, 1, q, half(b)], part_in.at[s, q, half(b)], gp_send.at[s, q, b], gp_recv.at[s, q, b], (iy, partner))

    chunks = [(q, b) for q in (0, 1) for b in (0, 1)]

    def start_own(s):
        for q, b in chunks:
            swap_copy(s, q, b).start()

    def start_own_edges(s):
        for q, b in chunks:
            pl.when(vertical[b][1])(lambda q=q, b=b: edge_copy(s, q, b, 0).start())

    def on_swap(s):
        for q, b in chunks:
            swap_copy(s, q, b).wait_recv()
            pl.when(has_target)(lambda q=q, b=b: relay_copy(s, q, b).start())
            pl.when(vertical[b][1])(lambda q=q, b=b: edge_copy(s, q, b, 1).start())

    def on_relay(s):
        @pl.when(has_source)
        def _():
            for q, b in chunks:
                relay_copy(s, q, b).wait_recv()
                pl.when(vertical[b][1])(lambda q=q, b=b: edge_copy(s, q, b, 2).start())

    def on_edges(s):
        for q, b in chunks:
            @pl.when(vertical[1 - b][1])
            def _(q=q, b=b):
                edge_copy(s, q, b, 0).wait_recv()
                edge_copy(s, q, b, 1).wait_recv()
                pl.when(has_source)(lambda: edge_copy(s, q, b, 2).wait_recv())

    def send_rows(s):
        for t in (2, 1, 0):
            for q, b in chunks:
                pl.when(vertical[1 - b][1])(lambda q=q, b=b, t=t: rows_copy(s, q, b, t).start())

    def add_rows(s, q, b, t):
        @pl.when(vertical[b][1])
        def _():
            rows_copy(s, q, b, t).wait_recv()
            g_tile[s, t, q, half(b), :] += rows_in[s, b, t, q]

    def send_far(s):
        @pl.when(has_source)
        def _():
            for q, b in chunks:
                add_rows(s, q, b, 2)
                far_copy(s, q, b).start()

        @pl.when(jnp.logical_not(has_source))
        def _():
            for q, b in chunks:
                add_rows(s, q, b, 2)

    def send_part(s):
        for q, b in chunks:
            add_rows(s, q, b, 1)

            @pl.when(has_target)
            def _(q=q, b=b):
                far_copy(s, q, b).wait_recv()
                g_tile[s, 1, q, half(b), :] += far_in[s, q, half(b), :]

            part_copy(s, q, b).start()

    def finish(s):
        for q, b in chunks:
            add_rows(s, q, b, 0)
            part_copy(s, q, b).wait_recv()
            out_ref[s, q, half(b), :] = g_tile[s, 0, q, half(b), :] + part_in[s, q, half(b), :]

    start_own(0)
    start_own_edges(0)
    start_own(1)
    start_own_edges(1)
    tr_ref[0] = jnp.cos(phase_ref[...])
    tr_ref[1] = jnp.sin(phase_ref[...])
    for p in range(count):
        r, c = lax.rem(sc_ref[p, 0], n), sc_ref[p, 1]
        roll_ref[p, 0] = pltpu.roll(pltpu.roll(probe_ref[0], c, 1), r, 0)
        roll_ref[p, 1] = pltpu.roll(pltpu.roll(probe_ref[1], c, 1), r, 0)
    g_tile[...] = jnp.zeros_like(g_tile)
    g_edge[...] = jnp.zeros_like(g_edge)
    for load in loads:
        load.wait()
    on_swap(0)
    on_relay(0)
    on_swap(1)
    on_edges(0)

    def first(p, carry):
        @pl.when(p == 1)
        def _():
            on_relay(1)

        mask = masks(sc_ref, p, n, odd)
        tiles = (own.at[0], part.at[0], far.at[0])
        wr = window(0, tiles, edge.at[0], mask, n)
        wi = window(1, tiles, edge.at[0], mask, n)
        xr, xi = fft2(*mul(roll_ref[p, 0], roll_ref[p, 1], wr, wi), right_ref, left_ref)
        xr, xi = ifft2(*mul(tr_ref[0], tr_ref[1], xr, xi), right_ref, left_ref)
        phi_ref[p, 0] = xr
        phi_ref[p, 1] = xi
        return carry

    lax.fori_loop(0, count, first, 0)
    if count == 1:
        on_relay(1)
    on_edges(1)

    def second(p, carry):
        mask = masks(sc_ref, p, n, odd)
        tiles = (own.at[1], part.at[1], far.at[1])
        wr = window(0, tiles, edge.at[1], mask, n)
        wi = window(1, tiles, edge.at[1], mask, n)
        fr, fi = fft2(*mul(phi_ref[p, 0], phi_ref[p, 1], wr, wi), right_ref, left_ref)
        res = 2.0 * (fr * fr + fi * fi - intensity_ref[p])
        br, bi = ifft2(res * fr, res * fi, right_ref, left_ref)
        zr, zi = mul(wr, -wi, br, bi)
        back_ref[p, 0] = zr
        back_ref[p, 1] = zi
        gr, gi = mul(phi_ref[p, 0], -phi_ref[p, 1], br, bi)
        scatter(gr, 0, g_tile.at[1], g_edge.at[1], mask, n)
        scatter(gi, 1, g_tile.at[1], g_edge.at[1], mask, n)
        return carry

    lax.fori_loop(0, count, second, 0)
    send_rows(1)

    def third(p, carry):
        mask = masks(sc_ref, p, n, odd)
        xr, xi = fft2(back_ref[p, 0], back_ref[p, 1], right_ref, left_ref)
        xr, xi = mul(tr_ref[0], -tr_ref[1], xr, xi)
        back_ref[p, 0] = xr
        back_ref[p, 1] = xi

        @pl.when(p == 0)
        def _():
            send_far(1)

        @pl.when(p == 1)
        def _():
            send_part(1)

        xr, xi = ifft2(back_ref[p, 0], back_ref[p, 1], right_ref, left_ref)
        gr, gi = mul(roll_ref[p, 0], -roll_ref[p, 1], xr, xi)
        scatter(gr, 0, g_tile.at[0], g_edge.at[0], mask, n)
        scatter(gi, 1, g_tile.at[0], g_edge.at[0], mask, n)
        return carry

    lax.fori_loop(0, count, third, 0)
    if count == 1:
        send_part(1)
    send_rows(0)
    send_far(0)
    send_part(0)
    finish(1)
    finish(0)
    for s in (0, 1):
        for q, b in chunks:
            swap_copy(s, q, b).wait_send()
            part_copy(s, q, b).wait_send()
            pl.when(has_target)(lambda s=s, q=q, b=b: relay_copy(s, q, b).wait_send())
            pl.when(has_source)(lambda s=s, q=q, b=b: far_copy(s, q, b).wait_send())

            @pl.when(vertical[b][1])
            def _(s=s, q=q, b=b):
                edge_copy(s, q, b, 0).wait_send()
                edge_copy(s, q, b, 1).wait_send()
                pl.when(has_source)(lambda: edge_copy(s, q, b, 2).wait_send())

            @pl.when(vertical[1 - b][1])
            def _(s=s, q=q, b=b):
                for t in (0, 1, 2):
                    rows_copy(s, q, b, t).wait_send()


def on_device(intensity, corner, probe, prop_phase, object_slices, momentum):
    count, n = intensity.shape[0], intensity.shape[-1]
    h = n // 2
    _, _, tile_rows, tile_cols = object_slices.shape
    assert tile_rows == n and tile_cols == h
    nty, ntx = lax.axis_size("ty"), lax.axis_size("tx")
    assert ntx % 2 == 0
    iy, ix = lax.axis_index("ty"), lax.axis_index("tx")
    sc = jnp.stack([corner[:, 0] - (iy * tile_rows - h), corner[:, 1] - (ix * tile_cols - h)], axis=1)
    right, left = dft_tables(n)
    f32 = jnp.float32
    field = pltpu.VMEM((count, 2, n, n), f32)
    dma = pltpu.SemaphoreType.DMA
    tiles, edges = (2, 2, n, h), (2, 2, 3, 2, h, h)
    gradient = pl.pallas_call(
        functools.partial(kernel, (nty, ntx)),
        out_shape=jax.ShapeDtypeStruct(object_slices.shape, f32),
        in_specs=[SMEM, VMEM, VMEM, VMEM, ANY, ANY, ANY],
        out_specs=VMEM,
        scratch_shapes=[
            pltpu.VMEM(right.shape, right.dtype),
            pltpu.VMEM(left.shape, left.dtype),
            pltpu.VMEM(intensity.shape, f32),
            pltpu.VMEM((2, n, n), f32),
            field,
            field,
            field,
            pltpu.VMEM(tiles, f32),
            pltpu.VMEM(tiles, f32),
            pltpu.VMEM(edges, f32),
            pltpu.VMEM((2, 3, 2, n, h), f32),
            pltpu.VMEM(edges, f32),
            pltpu.VMEM(edges, f32),
            pltpu.VMEM(tiles, f32),
            pltpu.VMEM(tiles, f32),
            dma((3,)),
        ]
        + [dma((2, 2, 2))] * 4
        + [dma((2, 2, 3, 2))] * 4
        + [dma((2, 2, 2))] * 4,
        compiler_params=pltpu.CompilerParams(
            collective_id=0, has_side_effects=True, vmem_limit_bytes=48 << 20
        ),
    )(sc, object_slices, probe, prop_phase, intensity, right, left)
    momentum_next = decay_rate * momentum + grad_scale * gradient
    object_next = object_slices - step_length * momentum_next
    return (object_next, momentum_next)


def solution(mesh):
    return jax.shard_map(
        on_device,
        mesh=mesh,
        in_specs=(
            P(("ty", "tx"), None, None),
            P(("ty", "tx"), None),
            P(),
            P(),
            P(None, None, "ty", "tx"),
            P(None, None, "ty", "tx"),
        ),
        out_specs=(P(None, None, "ty", "tx"), P(None, None, "ty", "tx")),
        check_vma=False,
    )
```

```python
import functools
import math

import jax
import jax.numpy as jnp
import numpy as np
from jax import lax
from jax.experimental import pallas as pl
from jax.experimental.pallas import tpu as pltpu
from jax.sharding import PartitionSpec as P

decay_rate = 0.9
grad_scale = 0.05
step_length = 0.5

VMEM = pl.BlockSpec(memory_space=pltpu.VMEM)
ANY = pl.BlockSpec(memory_space=pl.ANY)
SMEM = pl.BlockSpec(memory_space=pltpu.SMEM)


def dft_tables(n):
    k = np.arange(n)
    angle = 2.0 * math.pi * (np.outer(k, k) % n) / n
    c, s = np.cos(angle) / math.sqrt(n), -np.sin(angle) / math.sqrt(n)
    right = np.block([[c, s], [-s, c]]).astype(np.float32)
    left = np.concatenate([c, s], axis=0).astype(np.float32)

    def split(t):
        hi = t.astype(jnp.bfloat16)
        lo = (t - hi.astype(np.float32)).astype(jnp.bfloat16)
        return hi, lo

    rh, rl = split(right)
    lh, ll = split(left)
    return (
        jnp.asarray(np.concatenate([rh, rh, rl], axis=0)),
        jnp.asarray(np.concatenate([lh, lh, ll], axis=1)),
    )


def halves(x):
    hi = x.astype(jnp.bfloat16)
    lo = (x - hi.astype(jnp.float32)).astype(jnp.bfloat16)
    return hi, lo


def fft2(xr, xi, right_ref, left_ref):
    n = xr.shape[-1]
    hi, lo = halves(jnp.concatenate([xr, xi], axis=1))
    y = jnp.dot(
        jnp.concatenate([hi, lo, hi], axis=1), right_ref[...], preferred_element_type=jnp.float32
    )
    hi, lo = halves(y)
    z = jnp.dot(
        left_ref[...], jnp.concatenate([hi, lo, hi], axis=0), preferred_element_type=jnp.float32
    )
    return z[:n, :n] - z[n:, n:], z[:n, n:] + z[n:, :n]


def ifft2(xr, xi, right_ref, left_ref):
    yi, yr = fft2(xi, xr, right_ref, left_ref)
    return yr, yi


def mul(ar, ai, br, bi):
    return ar * br - ai * bi, ar * bi + ai * br


def masks(start, p, n, odd):
    r, c = start(p)
    h = n // 2
    rows = lax.broadcasted_iota(jnp.int32, (n, h), 0)
    cols = lax.broadcasted_iota(jnp.int32, (n, h), 1)
    later = (cols >= c).astype(jnp.int32)
    return rows >= r, (later + odd) == 1


def window(q, tiles, edge, mask, n):
    h = n // 2
    row_first, use_far = mask
    cols = []
    for t, tile in enumerate(tiles):
        top = jnp.where(row_first[:h], edge[1, t, q], tile[q, h:, :])
        bottom = jnp.where(row_first[h:], tile[q, :h, :], edge[0, t, q])
        cols.append(jnp.concatenate([top, bottom], axis=0))
    own, partner, far = cols
    return jnp.concatenate([jnp.where(use_far, far, partner), own], axis=1)


def scatter(g, q, g_tile, g_edge, mask, n):
    h = n // 2
    row_first, use_far = mask
    left, own = g[:, :h], g[:, h:]
    zero = jnp.zeros_like(left)
    parts = (own, jnp.where(use_far, zero, left), jnp.where(use_far, left, zero))
    for t, v in enumerate(parts):
        low = jnp.where(row_first, v, zero)
        high = jnp.where(row_first, zero, v)
        g_edge[1, t, q] += low[:h]
        g_tile[t, q, h:, :] += high[:h]
        g_tile[t, q, :h, :] += low[h:]
        g_edge[0, t, q] += high[h:]


def kernel(
    sizes, corner_ref, own_hbm, probe_hbm, phase_hbm, intensity_hbm, right_hbm, left_hbm, out_ref,
    own, probe_ref, phase_ref, right_ref, left_ref, intensity_ref, tr_ref, roll_ref, phi_ref, back_ref,
    part, far, edge, g_tile, g_edge, rows_in, far_in, part_in,
    local_sem, m_send, m_recv, f_send, f_recv, e_send, e_recv,
    r_send, r_recv, gf_send, gf_recv, gp_send, gp_recv,
):
    nty, ntx = sizes
    count, n = intensity_ref.shape[0], intensity_ref.shape[-1]
    h = n // 2
    iy, ix = lax.axis_index("ty"), lax.axis_index("tx")
    odd = lax.rem(ix, 2)
    partner = ix + 1 - 2 * odd
    target = ix + 2 - 4 * odd
    source = ix - 2 + 4 * odd
    has_target = jnp.logical_and(target >= 0, target < ntx)
    has_source = jnp.logical_and(source >= 0, source < ntx)
    has_up, has_down = iy > 0, iy < nty - 1
    vertical = ((iy - 1, has_up), (iy + 1, has_down))

    def start(p):
        return corner_ref[p, 0] - (iy * n - h), corner_ref[p, 1] - (ix * h - h)

    loads = [
        pltpu.make_async_copy(a, b, local_sem.at[i])
        for i, (a, b) in enumerate(
            (
                (own_hbm, own),
                (phase_hbm, phase_ref),
                (probe_hbm, probe_ref),
                (right_hbm, right_ref),
                (left_hbm, left_ref),
                (intensity_hbm, intensity_ref),
            )
        )
    ]
    for load in loads:
        load.start()

    barrier = pltpu.get_barrier_semaphore()

    def greet(dev):
        pl.semaphore_signal(barrier, inc=1, device_id=dev, device_id_type=pl.DeviceIdType.MESH)

    greet((iy, partner))
    for cond, dev in (
        (has_target, (iy, target)),
        (has_source, (iy, source)),
        (has_up, (iy - 1, ix)),
        (has_down, (iy + 1, ix)),
    ):
        pl.when(cond)(functools.partial(greet, dev))
    peers = 1 + sum(cond.astype(jnp.int32) for cond in (has_target, has_source, has_up, has_down))
    pl.semaphore_wait(barrier, peers)

    def remote(src, dst, send, recv, dev):
        return pltpu.make_async_remote_copy(
            src_ref=src, dst_ref=dst, send_sem=send, recv_sem=recv,
            device_id=dev, device_id_type=pl.DeviceIdType.MESH,
        )

    def half(b):
        return pl.ds(b * h, h)

    def swap_copy(s, q, b):
        return remote(own.at[s, q, half(b)], part.at[s, q, half(b)], m_send.at[s, q, b], m_recv.at[s, q, b], (iy, partner))

    def relay_copy(s, q, b):
        return remote(part.at[s, q, half(b)], far.at[s, q, half(b)], f_send.at[s, q, b], f_recv.at[s, q, b], (iy, target))

    def edge_copy(s, q, b, t):
        src = (own, part, far)[t]
        return remote(src.at[s, q, half(b)], edge.at[s, b, t, q], e_send.at[s, b, t, q], e_recv.at[s, b, t, q], (vertical[b][0], ix))

    def rows_copy(s, q, b, t):
        return remote(g_edge.at[s, b, t, q], rows_in.at[s, b, t, q], r_send.at[s, b, t, q], r_recv.at[s, b, t, q], (vertical[1 - b][0], ix))

    def far_copy(s, q, b):
        return remote(g_tile.at[s, 2, q, half(b)], far_in.at[s, q, half(b)], gf_send.at[s, q, b], gf_recv.at[s, q, b], (iy, source))

    def part_copy(s, q, b):
        return remote(g_tile.at[s, 1, q, half(b)], part_in.at[s, q, half(b)], gp_send.at[s, q, b], gp_recv.at[s, q, b], (iy, partner))

    chunks = [(q, b) for q in (0, 1) for b in (0, 1)]

    def start_own(s):
        for q, b in chunks:
            swap_copy(s, q, b).start()

    def start_own_edges(s):
        for q, b in chunks:
            pl.when(vertical[b][1])(lambda q=q, b=b: edge_copy(s, q, b, 0).start())

    def on_swap(s):
        for q, b in chunks:
            swap_copy(s, q, b).wait_recv()
            pl.when(has_target)(lambda q=q, b=b: relay_copy(s, q, b).start())
            pl.when(vertical[b][1])(lambda q=q, b=b: edge_copy(s, q, b, 1).start())

    def on_relay(s):
        @pl.when(has_source)
        def _():
            for q, b in chunks:
                relay_copy(s, q, b).wait_recv()
                pl.when(vertical[b][1])(lambda q=q, b=b: edge_copy(s, q, b, 2).start())

    def on_edges(s):
        for q, b in chunks:
            @pl.when(vertical[1 - b][1])
            def _(q=q, b=b):
                edge_copy(s, q, b, 0).wait_recv()
                edge_copy(s, q, b, 1).wait_recv()
                pl.when(has_source)(lambda: edge_copy(s, q, b, 2).wait_recv())

    def send_rows(s):
        for t in (2, 1, 0):
            for q, b in chunks:
                pl.when(vertical[1 - b][1])(lambda q=q, b=b, t=t: rows_copy(s, q, b, t).start())

    def add_rows(s, q, b, t):
        @pl.when(vertical[b][1])
        def _():
            rows_copy(s, q, b, t).wait_recv()
            g_tile[s, t, q, half(b), :] += rows_in[s, b, t, q]

    def send_far(s):
        @pl.when(has_source)
        def _():
            for q, b in chunks:
                add_rows(s, q, b, 2)
                far_copy(s, q, b).start()

        @pl.when(jnp.logical_not(has_source))
        def _():
            for q, b in chunks:
                add_rows(s, q, b, 2)

    def send_part(s):
        for q, b in chunks:
            add_rows(s, q, b, 1)

            @pl.when(has_target)
            def _(q=q, b=b):
                far_copy(s, q, b).wait_recv()
                g_tile[s, 1, q, half(b), :] += far_in[s, q, half(b), :]

            part_copy(s, q, b).start()

    def finish(s):
        for q, b in chunks:
            add_rows(s, q, b, 0)
            part_copy(s, q, b).wait_recv()
            out_ref[s, q, half(b), :] = g_tile[s, 0, q, half(b), :] + part_in[s, q, half(b), :]

    loads[0].wait()
    start_own(0)
    start_own_edges(0)
    start_own(1)
    start_own_edges(1)
    loads[1].wait()
    loads[2].wait()
    tr_ref[0] = jnp.cos(phase_ref[...])
    tr_ref[1] = jnp.sin(phase_ref[...])
    for p in range(count):
        r, c = start(p)
        r = lax.rem(r, n)
        roll_ref[p, 0] = pltpu.roll(pltpu.roll(probe_ref[0], c, 1), r, 0)
        roll_ref[p, 1] = pltpu.roll(pltpu.roll(probe_ref[1], c, 1), r, 0)
    g_tile[...] = jnp.zeros_like(g_tile)
    g_edge[...] = jnp.zeros_like(g_edge)
    for load in loads[3:]:
        load.wait()
    on_swap(0)
    on_relay(0)
    on_swap(1)
    on_edges(0)

    def first(p, carry):
        @pl.when(p == 1)
        def _():
            on_relay(1)

        mask = masks(start, p, n, odd)
        tiles = (own.at[0], part.at[0], far.at[0])
        wr = window(0, tiles, edge.at[0], mask, n)
        wi = window(1, tiles, edge.at[0], mask, n)
        xr, xi = fft2(*mul(roll_ref[p, 0], roll_ref[p, 1], wr, wi), right_ref, left_ref)
        xr, xi = ifft2(*mul(tr_ref[0], tr_ref[1], xr, xi), right_ref, left_ref)
        phi_ref[p, 0] = xr
        phi_ref[p, 1] = xi
        return carry

    lax.fori_loop(0, count, first, 0)
    if count == 1:
        on_relay(1)
    on_edges(1)

    def second(p, carry):
        mask = masks(start, p, n, odd)
        tiles = (own.at[1], part.at[1], far.at[1])
        wr = window(0, tiles, edge.at[1], mask, n)
        wi = window(1, tiles, edge.at[1], mask, n)
        fr, fi = fft2(*mul(phi_ref[p, 0], phi_ref[p, 1], wr, wi), right_ref, left_ref)
        res = 2.0 * (fr * fr + fi * fi - intensity_ref[p])
        br, bi = ifft2(res * fr, res * fi, right_ref, left_ref)
        zr, zi = mul(wr, -wi, br, bi)
        back_ref[p, 0] = zr
        back_ref[p, 1] = zi
        gr, gi = mul(phi_ref[p, 0], -phi_ref[p, 1], br, bi)
        scatter(gr, 0, g_tile.at[1], g_edge.at[1], mask, n)
        scatter(gi, 1, g_tile.at[1], g_edge.at[1], mask, n)
        return carry

    lax.fori_loop(0, count, second, 0)
    send_rows(1)

    def third(p, carry):
        mask = masks(start, p, n, odd)
        xr, xi = fft2(back_ref[p, 0], back_ref[p, 1], right_ref, left_ref)
        xr, xi = mul(tr_ref[0], -tr_ref[1], xr, xi)
        back_ref[p, 0] = xr
        back_ref[p, 1] = xi

        @pl.when(p == 0)
        def _():
            send_far(1)

        @pl.when(p == 1)
        def _():
            send_part(1)

        xr, xi = ifft2(back_ref[p, 0], back_ref[p, 1], right_ref, left_ref)
        gr, gi = mul(roll_ref[p, 0], -roll_ref[p, 1], xr, xi)
        scatter(gr, 0, g_tile.at[0], g_edge.at[0], mask, n)
        scatter(gi, 1, g_tile.at[0], g_edge.at[0], mask, n)
        return carry

    lax.fori_loop(0, count, third, 0)
    if count == 1:
        send_part(1)
    send_rows(0)
    send_far(0)
    send_part(0)
    finish(1)
    finish(0)
    for s in (0, 1):
        for q, b in chunks:
            swap_copy(s, q, b).wait_send()
            part_copy(s, q, b).wait_send()
            pl.when(has_target)(lambda s=s, q=q, b=b: relay_copy(s, q, b).wait_send())
            pl.when(has_source)(lambda s=s, q=q, b=b: far_copy(s, q, b).wait_send())

            @pl.when(vertical[b][1])
            def _(s=s, q=q, b=b):
                edge_copy(s, q, b, 0).wait_send()
                edge_copy(s, q, b, 1).wait_send()
                pl.when(has_source)(lambda: edge_copy(s, q, b, 2).wait_send())

            @pl.when(vertical[1 - b][1])
            def _(s=s, q=q, b=b):
                for t in (0, 1, 2):
                    rows_copy(s, q, b, t).wait_send()


def on_device(intensity, corner, probe, prop_phase, object_slices, momentum):
    count, n = intensity.shape[0], intensity.shape[-1]
    h = n // 2
    _, _, tile_rows, tile_cols = object_slices.shape
    assert tile_rows == n and tile_cols == h
    nty, ntx = lax.axis_size("ty"), lax.axis_size("tx")
    assert ntx % 2 == 0
    right, left = dft_tables(n)
    f32 = jnp.float32
    field = pltpu.VMEM((count, 2, n, n), f32)
    dma = pltpu.SemaphoreType.DMA
    tiles, edges = (2, 2, n, h), (2, 2, 3, 2, h, h)
    gradient = pl.pallas_call(
        functools.partial(kernel, (nty, ntx)),
        out_shape=jax.ShapeDtypeStruct(object_slices.shape, f32),
        in_specs=[SMEM] + [ANY] * 6,
        out_specs=VMEM,
        scratch_shapes=[
            pltpu.VMEM(object_slices.shape, f32),
            pltpu.VMEM(probe.shape, f32),
            pltpu.VMEM(prop_phase.shape, f32),
            pltpu.VMEM(right.shape, right.dtype),
            pltpu.VMEM(left.shape, left.dtype),
            pltpu.VMEM(intensity.shape, f32),
            pltpu.VMEM((2, n, n), f32),
            field,
            field,
            field,
            pltpu.VMEM(tiles, f32),
            pltpu.VMEM(tiles, f32),
            pltpu.VMEM(edges, f32),
            pltpu.VMEM((2, 3, 2, n, h), f32),
            pltpu.VMEM(edges, f32),
            pltpu.VMEM(edges, f32),
            pltpu.VMEM(tiles, f32),
            pltpu.VMEM(tiles, f32),
            dma((6,)),
        ]
        + [dma((2, 2, 2))] * 4
        + [dma((2, 2, 3, 2))] * 4
        + [dma((2, 2, 2))] * 4,
        compiler_params=pltpu.CompilerParams(
            collective_id=0, has_side_effects=True, vmem_limit_bytes=67043328
        ),
    )(corner, object_slices, probe, prop_phase, intensity, right, left)
    momentum_next = decay_rate * momentum + grad_scale * gradient
    object_next = object_slices - step_length * momentum_next
    return (object_next, momentum_next)


def solution(mesh):
    return jax.shard_map(
        on_device,
        mesh=mesh,
        in_specs=(
            P(("ty", "tx"), None, None),
            P(("ty", "tx"), None),
            P(),
            P(),
            P(None, None, "ty", "tx"),
            P(None, None, "ty", "tx"),
        ),
        out_specs=(P(None, None, "ty", "tx"), P(None, None, "ty", "tx")),
        check_vma=False,
    )
```

```python
import functools
import math

import jax
import jax.numpy as jnp
import numpy as np
from jax import lax
from jax.experimental import pallas as pl
from jax.experimental.pallas import tpu as pltpu
from jax.sharding import PartitionSpec as P

decay_rate = 0.9
grad_scale = 0.05
step_length = 0.5

VMEM = pl.BlockSpec(memory_space=pltpu.VMEM)
ANY = pl.BlockSpec(memory_space=pl.ANY)
SMEM = pl.BlockSpec(memory_space=pltpu.SMEM)


def dft_tables(n):
    k = np.arange(n)
    angle = 2.0 * math.pi * (np.outer(k, k) % n) / n
    c, s = np.cos(angle) / math.sqrt(n), -np.sin(angle) / math.sqrt(n)
    right = np.block([[c, s], [-s, c]]).astype(np.float32)
    left = np.concatenate([c, s], axis=0).astype(np.float32)

    def split(t):
        hi = t.astype(jnp.bfloat16)
        lo = (t - hi.astype(np.float32)).astype(jnp.bfloat16)
        return hi, lo

    rh, rl = split(right)
    lh, ll = split(left)
    return (
        jnp.asarray(np.concatenate([rh, rh, rl], axis=0)),
        jnp.asarray(np.concatenate([lh, lh, ll], axis=1)),
    )


def halves(x):
    hi = x.astype(jnp.bfloat16)
    lo = (x - hi.astype(jnp.float32)).astype(jnp.bfloat16)
    return hi, lo


def fft2(xr, xi, right_ref, left_ref):
    n = xr.shape[-1]
    hi, lo = halves(jnp.concatenate([xr, xi], axis=1))
    y = jnp.dot(
        jnp.concatenate([hi, lo, hi], axis=1), right_ref[...], preferred_element_type=jnp.float32
    )
    hi, lo = halves(y)
    z = jnp.dot(
        left_ref[...], jnp.concatenate([hi, lo, hi], axis=0), preferred_element_type=jnp.float32
    )
    return z[:n, :n] - z[n:, n:], z[:n, n:] + z[n:, :n]


def ifft2(xr, xi, right_ref, left_ref):
    yi, yr = fft2(xi, xr, right_ref, left_ref)
    return yr, yi


def mul(ar, ai, br, bi):
    return ar * br - ai * bi, ar * bi + ai * br


def masks(start, p, n, odd):
    r, c = start(p)
    h = n // 2
    rows = lax.broadcasted_iota(jnp.int32, (n, h), 0)
    cols = lax.broadcasted_iota(jnp.int32, (n, h), 1)
    later = (cols >= c).astype(jnp.int32)
    return rows >= r, (later + odd) == 1


def window(q, tiles, edge, mask, n):
    h = n // 2
    row_first, use_far = mask
    cols = []
    for t, tile in enumerate(tiles):
        top = jnp.where(row_first[:h], edge[1, t, q], tile[q, h:, :])
        bottom = jnp.where(row_first[h:], tile[q, :h, :], edge[0, t, q])
        cols.append(jnp.concatenate([top, bottom], axis=0))
    own, partner, far = cols
    return jnp.concatenate([jnp.where(use_far, far, partner), own], axis=1)


def scatter(g, q, g_tile, g_edge, mask, n):
    h = n // 2
    row_first, use_far = mask
    left, own = g[:, :h], g[:, h:]
    zero = jnp.zeros_like(left)
    parts = (own, jnp.where(use_far, zero, left), jnp.where(use_far, left, zero))
    for t, v in enumerate(parts):
        low = jnp.where(row_first, v, zero)
        high = jnp.where(row_first, zero, v)
        g_edge[1, t, q] += low[:h]
        g_tile[t, q, h:, :] += high[:h]
        g_tile[t, q, :h, :] += low[h:]
        g_edge[0, t, q] += high[h:]


def kernel(
    sizes, corner_ref, own_hbm, probe_hbm, phase_hbm, intensity_hbm, right_hbm, left_hbm, out_ref,
    own, probe_ref, phase_ref, right_ref, left_ref, intensity_ref, tr_ref, roll_ref, phi_ref, back_ref,
    part, far, edge, g_tile, g_edge, rows_in, far_in, part_in,
    local_sem, m_send, m_recv, f_send, f_recv, e_send, e_recv,
    r_send, r_recv, gf_send, gf_recv, gp_send, gp_recv,
):
    nty, ntx = sizes
    count, n = intensity_ref.shape[0], intensity_ref.shape[-1]
    h = n // 2
    iy, ix = lax.axis_index("ty"), lax.axis_index("tx")
    odd = lax.rem(ix, 2)
    partner = ix + 1 - 2 * odd
    target = ix + 2 - 4 * odd
    source = ix - 2 + 4 * odd
    has_target = jnp.logical_and(target >= 0, target < ntx)
    has_source = jnp.logical_and(source >= 0, source < ntx)
    has_up, has_down = iy > 0, iy < nty - 1
    vertical = ((iy - 1, has_up), (iy + 1, has_down))

    def start(p):
        return corner_ref[p, 0] - (iy * n - h), corner_ref[p, 1] - (ix * h - h)

    loads = [
        pltpu.make_async_copy(a, b, local_sem.at[i])
        for i, (a, b) in enumerate(
            (
                (own_hbm, own),
                (phase_hbm, phase_ref),
                (probe_hbm, probe_ref),
                (right_hbm, right_ref),
                (left_hbm, left_ref),
                (intensity_hbm, intensity_ref),
            )
        )
    ]
    for load in loads:
        load.start()

    barrier = pltpu.get_barrier_semaphore()

    def greet(dev):
        pl.semaphore_signal(barrier, inc=1, device_id=dev, device_id_type=pl.DeviceIdType.MESH)

    greet((iy, partner))
    for cond, dev in (
        (has_target, (iy, target)),
        (has_source, (iy, source)),
        (has_up, (iy - 1, ix)),
        (has_down, (iy + 1, ix)),
    ):
        pl.when(cond)(functools.partial(greet, dev))
    peers = 1 + sum(cond.astype(jnp.int32) for cond in (has_target, has_source, has_up, has_down))
    pl.semaphore_wait(barrier, peers)

    def remote(src, dst, send, recv, dev):
        return pltpu.make_async_remote_copy(
            src_ref=src, dst_ref=dst, send_sem=send, recv_sem=recv,
            device_id=dev, device_id_type=pl.DeviceIdType.MESH,
        )

    def half(b):
        return pl.ds(b * h, h)

    def swap_copy(s, q, b):
        return remote(own_hbm.at[s, q, half(b)], part.at[s, q, half(b)], m_send.at[s, q, b], m_recv.at[s, q, b], (iy, partner))

    def relay_copy(s, q, b):
        return remote(part.at[s, q, half(b)], far.at[s, q, half(b)], f_send.at[s, q, b], f_recv.at[s, q, b], (iy, target))

    def edge_copy(s, q, b, t):
        src = (own_hbm, part, far)[t]
        return remote(src.at[s, q, half(b)], edge.at[s, b, t, q], e_send.at[s, b, t, q], e_recv.at[s, b, t, q], (vertical[b][0], ix))

    def rows_copy(s, q, b, t):
        return remote(g_edge.at[s, b, t, q], rows_in.at[s, b, t, q], r_send.at[s, b, t, q], r_recv.at[s, b, t, q], (vertical[1 - b][0], ix))

    def far_copy(s, q, b):
        return remote(g_tile.at[s, 2, q, half(b)], far_in.at[s, q, half(b)], gf_send.at[s, q, b], gf_recv.at[s, q, b], (iy, source))

    def part_copy(s, q, b):
        return remote(g_tile.at[s, 1, q, half(b)], part_in.at[s, q, half(b)], gp_send.at[s, q, b], gp_recv.at[s, q, b], (iy, partner))

    chunks = [(q, b) for q in (0, 1) for b in (0, 1)]

    def start_own(s):
        for q, b in chunks:
            swap_copy(s, q, b).start()

    def start_own_edges(s):
        for q, b in chunks:
            pl.when(vertical[b][1])(lambda q=q, b=b: edge_copy(s, q, b, 0).start())

    def on_swap(s):
        for q, b in chunks:
            swap_copy(s, q, b).wait_recv()
            pl.when(has_target)(lambda q=q, b=b: relay_copy(s, q, b).start())
            pl.when(vertical[b][1])(lambda q=q, b=b: edge_copy(s, q, b, 1).start())

    def on_relay(s):
        @pl.when(has_source)
        def _():
            for q, b in chunks:
                relay_copy(s, q, b).wait_recv()
                pl.when(vertical[b][1])(lambda q=q, b=b: edge_copy(s, q, b, 2).start())

    def on_edges(s):
        for q, b in chunks:
            @pl.when(vertical[1 - b][1])
            def _(q=q, b=b):
                edge_copy(s, q, b, 0).wait_recv()
                edge_copy(s, q, b, 1).wait_recv()
                pl.when(has_source)(lambda: edge_copy(s, q, b, 2).wait_recv())

    def send_rows(s):
        for t in (2, 1, 0):
            for q, b in chunks:
                pl.when(vertical[1 - b][1])(lambda q=q, b=b, t=t: rows_copy(s, q, b, t).start())

    def add_rows(s, q, b, t):
        @pl.when(vertical[b][1])
        def _():
            rows_copy(s, q, b, t).wait_recv()
            g_tile[s, t, q, half(b), :] += rows_in[s, b, t, q]

    def send_far(s):
        @pl.when(has_source)
        def _():
            for q, b in chunks:
                add_rows(s, q, b, 2)
                far_copy(s, q, b).start()

        @pl.when(jnp.logical_not(has_source))
        def _():
            for q, b in chunks:
                add_rows(s, q, b, 2)

    def send_part(s):
        for q, b in chunks:
            add_rows(s, q, b, 1)

            @pl.when(has_target)
            def _(q=q, b=b):
                far_copy(s, q, b).wait_recv()
                g_tile[s, 1, q, half(b), :] += far_in[s, q, half(b), :]

            part_copy(s, q, b).start()

    def finish(s):
        for q, b in chunks:
            add_rows(s, q, b, 0)
            part_copy(s, q, b).wait_recv()
            out_ref[s, q, half(b), :] = g_tile[s, 0, q, half(b), :] + part_in[s, q, half(b), :]

    start_own(0)
    start_own_edges(0)
    start_own(1)
    start_own_edges(1)
    loads[1].wait()
    loads[2].wait()
    tr_ref[0] = jnp.cos(phase_ref[...])
    tr_ref[1] = jnp.sin(phase_ref[...])
    for p in range(count):
        r, c = start(p)
        r = lax.rem(r, n)
        roll_ref[p, 0] = pltpu.roll(pltpu.roll(probe_ref[0], c, 1), r, 0)
        roll_ref[p, 1] = pltpu.roll(pltpu.roll(probe_ref[1], c, 1), r, 0)
    g_tile[...] = jnp.zeros_like(g_tile)
    g_edge[...] = jnp.zeros_like(g_edge)
    for load in (loads[0], *loads[3:]):
        load.wait()
    on_swap(0)
    on_relay(0)
    on_swap(1)
    on_edges(0)

    def first(p, carry):
        @pl.when(p == 1)
        def _():
            on_relay(1)

        mask = masks(start, p, n, odd)
        tiles = (own.at[0], part.at[0], far.at[0])
        wr = window(0, tiles, edge.at[0], mask, n)
        wi = window(1, tiles, edge.at[0], mask, n)
        xr, xi = fft2(*mul(roll_ref[p, 0], roll_ref[p, 1], wr, wi), right_ref, left_ref)
        xr, xi = ifft2(*mul(tr_ref[0], tr_ref[1], xr, xi), right_ref, left_ref)
        phi_ref[p, 0] = xr
        phi_ref[p, 1] = xi
        return carry

    lax.fori_loop(0, count, first, 0)
    if count == 1:
        on_relay(1)
    on_edges(1)

    def second(p, carry):
        mask = masks(start, p, n, odd)
        tiles = (own.at[1], part.at[1], far.at[1])
        wr = window(0, tiles, edge.at[1], mask, n)
        wi = window(1, tiles, edge.at[1], mask, n)
        fr, fi = fft2(*mul(phi_ref[p, 0], phi_ref[p, 1], wr, wi), right_ref, left_ref)
        res = 2.0 * (fr * fr + fi * fi - intensity_ref[p])
        br, bi = ifft2(res * fr, res * fi, right_ref, left_ref)
        zr, zi = mul(wr, -wi, br, bi)
        back_ref[p, 0] = zr
        back_ref[p, 1] = zi
        gr, gi = mul(phi_ref[p, 0], -phi_ref[p, 1], br, bi)
        scatter(gr, 0, g_tile.at[1], g_edge.at[1], mask, n)
        scatter(gi, 1, g_tile.at[1], g_edge.at[1], mask, n)
        return carry

    lax.fori_loop(0, count, second, 0)
    send_rows(1)

    def third(p, carry):
        @pl.when(p == 1)
        def _():
            send_far(1)

        mask = masks(start, p, n, odd)
        xr, xi = fft2(back_ref[p, 0], back_ref[p, 1], right_ref, left_ref)
        xr, xi = ifft2(*mul(tr_ref[0], -tr_ref[1], xr, xi), right_ref, left_ref)
        gr, gi = mul(roll_ref[p, 0], -roll_ref[p, 1], xr, xi)
        scatter(gr, 0, g_tile.at[0], g_edge.at[0], mask, n)
        scatter(gi, 1, g_tile.at[0], g_edge.at[0], mask, n)
        return carry

    lax.fori_loop(0, count, third, 0)
    send_rows(0)
    if count == 1:
        send_far(1)
    send_part(1)
    send_far(0)
    send_part(0)
    finish(1)
    finish(0)
    for s in (0, 1):
        for q, b in chunks:
            swap_copy(s, q, b).wait_send()
            part_copy(s, q, b).wait_send()
            pl.when(has_target)(lambda s=s, q=q, b=b: relay_copy(s, q, b).wait_send())
            pl.when(has_source)(lambda s=s, q=q, b=b: far_copy(s, q, b).wait_send())

            @pl.when(vertical[b][1])
            def _(s=s, q=q, b=b):
                edge_copy(s, q, b, 0).wait_send()
                edge_copy(s, q, b, 1).wait_send()
                pl.when(has_source)(lambda: edge_copy(s, q, b, 2).wait_send())

            @pl.when(vertical[1 - b][1])
            def _(s=s, q=q, b=b):
                for t in (0, 1, 2):
                    rows_copy(s, q, b, t).wait_send()


def on_device(intensity, corner, probe, prop_phase, object_slices, momentum):
    count, n = intensity.shape[0], intensity.shape[-1]
    h = n // 2
    _, _, tile_rows, tile_cols = object_slices.shape
    assert tile_rows == n and tile_cols == h
    nty, ntx = lax.axis_size("ty"), lax.axis_size("tx")
    assert ntx % 2 == 0
    right, left = dft_tables(n)
    f32 = jnp.float32
    field = pltpu.VMEM((count, 2, n, n), f32)
    dma = pltpu.SemaphoreType.DMA
    tiles, edges = (2, 2, n, h), (2, 2, 3, 2, h, h)
    gradient = pl.pallas_call(
        functools.partial(kernel, (nty, ntx)),
        out_shape=jax.ShapeDtypeStruct(object_slices.shape, f32),
        in_specs=[SMEM] + [ANY] * 6,
        out_specs=VMEM,
        scratch_shapes=[
            pltpu.VMEM(object_slices.shape, f32),
            pltpu.VMEM(probe.shape, f32),
            pltpu.VMEM(prop_phase.shape, f32),
            pltpu.VMEM(right.shape, right.dtype),
            pltpu.VMEM(left.shape, left.dtype),
            pltpu.VMEM(intensity.shape, f32),
            pltpu.VMEM((2, n, n), f32),
            field,
            field,
            field,
            pltpu.VMEM(tiles, f32),
            pltpu.VMEM(tiles, f32),
            pltpu.VMEM(edges, f32),
            pltpu.VMEM((2, 3, 2, n, h), f32),
            pltpu.VMEM(edges, f32),
            pltpu.VMEM(edges, f32),
            pltpu.VMEM(tiles, f32),
            pltpu.VMEM(tiles, f32),
            dma((6,)),
        ]
        + [dma((2, 2, 2))] * 4
        + [dma((2, 2, 3, 2))] * 4
        + [dma((2, 2, 2))] * 4,
        compiler_params=pltpu.CompilerParams(
            collective_id=0, has_side_effects=True, vmem_limit_bytes=67043328
        ),
    )(corner, object_slices, probe, prop_phase, intensity, right, left)
    momentum_next = decay_rate * momentum + grad_scale * gradient
    object_next = object_slices - step_length * momentum_next
    return (object_next, momentum_next)


def solution(mesh):
    return jax.shard_map(
        on_device,
        mesh=mesh,
        in_specs=(
            P(("ty", "tx"), None, None),
            P(("ty", "tx"), None),
            P(),
            P(),
            P(None, None, "ty", "tx"),
            P(None, None, "ty", "tx"),
        ),
        out_specs=(P(None, None, "ty", "tx"), P(None, None, "ty", "tx")),
        check_vma=False,
    )
```

```python
import functools
import math

import jax
import jax.numpy as jnp
import numpy as np
from jax import lax
from jax.experimental import pallas as pl
from jax.experimental.pallas import tpu as pltpu
from jax.sharding import PartitionSpec as P

decay_rate = 0.9
grad_scale = 0.05
step_length = 0.5

VMEM = pl.BlockSpec(memory_space=pltpu.VMEM)
ANY = pl.BlockSpec(memory_space=pl.ANY)
SMEM = pl.BlockSpec(memory_space=pltpu.SMEM)


def dft_tables(n):
    k = np.arange(n)
    angle = 2.0 * math.pi * (np.outer(k, k) % n) / n
    c, s = np.cos(angle) / math.sqrt(n), -np.sin(angle) / math.sqrt(n)
    right = np.block([[c, s], [-s, c]]).astype(np.float32)
    left = np.concatenate([c, s], axis=0).astype(np.float32)

    def split(t):
        hi = t.astype(jnp.bfloat16)
        lo = (t - hi.astype(np.float32)).astype(jnp.bfloat16)
        return hi, lo

    rh, rl = split(right)
    lh, ll = split(left)
    return (
        jnp.asarray(np.concatenate([rh, rh, rl], axis=0)),
        jnp.asarray(np.concatenate([lh, lh, ll], axis=1)),
    )


def halves(x):
    hi = x.astype(jnp.bfloat16)
    lo = (x - hi.astype(jnp.float32)).astype(jnp.bfloat16)
    return hi, lo


def fft2(xr, xi, right_ref, left_ref):
    n = xr.shape[-1]
    hi, lo = halves(jnp.concatenate([xr, xi], axis=1))
    y = jnp.dot(
        jnp.concatenate([hi, lo, hi], axis=1), right_ref[...], preferred_element_type=jnp.float32
    )
    hi, lo = halves(y)
    z = jnp.dot(
        left_ref[...], jnp.concatenate([hi, lo, hi], axis=0), preferred_element_type=jnp.float32
    )
    return z[:n, :n] - z[n:, n:], z[:n, n:] + z[n:, :n]


def ifft2(xr, xi, right_ref, left_ref):
    yi, yr = fft2(xi, xr, right_ref, left_ref)
    return yr, yi


def mul(ar, ai, br, bi):
    return ar * br - ai * bi, ar * bi + ai * br


def masks(start, p, n, odd):
    r, c = start(p)
    h = n // 2
    rows = lax.broadcasted_iota(jnp.int32, (n, h), 0)
    cols = lax.broadcasted_iota(jnp.int32, (n, h), 1)
    later = (cols >= c).astype(jnp.int32)
    return rows >= r, (later + odd) == 1


def window(q, tiles, edge, mask, n):
    h = n // 2
    row_first, use_far = mask
    cols = []
    for t, tile in enumerate(tiles):
        top = jnp.where(row_first[:h], edge[1, t, q], tile[q, h:, :])
        bottom = jnp.where(row_first[h:], tile[q, :h, :], edge[0, t, q])
        cols.append(jnp.concatenate([top, bottom], axis=0))
    own, partner, far = cols
    return jnp.concatenate([jnp.where(use_far, far, partner), own], axis=1)


def scatter(g, q, g_tile, g_edge, mask, n):
    h = n // 2
    row_first, use_far = mask
    left, own = g[:, :h], g[:, h:]
    zero = jnp.zeros_like(left)
    parts = (own, jnp.where(use_far, zero, left), jnp.where(use_far, left, zero))
    for t, v in enumerate(parts):
        low = jnp.where(row_first, v, zero)
        high = jnp.where(row_first, zero, v)
        g_edge[1, t, q] += low[:h]
        g_tile[t, q, h:, :] += high[:h]
        g_tile[t, q, :h, :] += low[h:]
        g_edge[0, t, q] += high[h:]


def kernel(
    sizes, corner_ref, own_hbm, probe_hbm, phase_hbm, intensity_hbm, right_hbm, left_hbm, out_ref,
    own, probe_ref, phase_ref, right_ref, left_ref, intensity_ref, tr_ref, roll_ref, phi_ref, back_ref,
    part, far, edge, g_tile, g_edge, rows_in, far_in, part_in,
    local_sem, m_send, m_recv, f_send, f_recv, e_send, e_recv,
    r_send, r_recv, gf_send, gf_recv, gp_send, gp_recv,
):
    nty, ntx = sizes
    count, n = intensity_ref.shape[0], intensity_ref.shape[-1]
    h = n // 2
    iy, ix = lax.axis_index("ty"), lax.axis_index("tx")
    odd = lax.rem(ix, 2)
    partner = ix + 1 - 2 * odd
    target = ix + 2 - 4 * odd
    source = ix - 2 + 4 * odd
    has_target = jnp.logical_and(target >= 0, target < ntx)
    has_source = jnp.logical_and(source >= 0, source < ntx)
    has_up, has_down = iy > 0, iy < nty - 1
    vertical = ((iy - 1, has_up), (iy + 1, has_down))

    def start(p):
        return corner_ref[p, 0] - (iy * n - h), corner_ref[p, 1] - (ix * h - h)

    loads = [
        pltpu.make_async_copy(a, b, local_sem.at[i])
        for i, (a, b) in enumerate(
            (
                (own_hbm, own),
                (phase_hbm, phase_ref),
                (probe_hbm, probe_ref),
                (right_hbm, right_ref),
                (left_hbm, left_ref),
                (intensity_hbm, intensity_ref),
            )
        )
    ]
    for load in loads:
        load.start()

    barrier = pltpu.get_barrier_semaphore()

    def greet(dev):
        pl.semaphore_signal(barrier, inc=1, device_id=dev, device_id_type=pl.DeviceIdType.MESH)

    greet((iy, partner))
    for cond, dev in (
        (has_target, (iy, target)),
        (has_source, (iy, source)),
        (has_up, (iy - 1, ix)),
        (has_down, (iy + 1, ix)),
    ):
        pl.when(cond)(functools.partial(greet, dev))
    peers = 1 + sum(cond.astype(jnp.int32) for cond in (has_target, has_source, has_up, has_down))
    pl.semaphore_wait(barrier, peers)

    def remote(src, dst, send, recv, dev):
        return pltpu.make_async_remote_copy(
            src_ref=src, dst_ref=dst, send_sem=send, recv_sem=recv,
            device_id=dev, device_id_type=pl.DeviceIdType.MESH,
        )

    def half(b):
        return pl.ds(b * h, h)

    def swap_copy(s, q, b):
        return remote(own_hbm.at[s, q, half(b)], part.at[s, q, half(b)], m_send.at[s, q, b], m_recv.at[s, q, b], (iy, partner))

    def relay_copy(s, q, b):
        return remote(part.at[s, q, half(b)], far.at[s, q, half(b)], f_send.at[s, q, b], f_recv.at[s, q, b], (iy, target))

    def edge_copy(s, q, b, t):
        src = (own_hbm, part, far)[t]
        return remote(src.at[s, q, half(b)], edge.at[s, b, t, q], e_send.at[s, b, t, q], e_recv.at[s, b, t, q], (vertical[b][0], ix))

    def rows_copy(s, q, b, t):
        return remote(g_edge.at[s, b, t, q], rows_in.at[s, b, t, q], r_send.at[s, b, t, q], r_recv.at[s, b, t, q], (vertical[1 - b][0], ix))

    def far_copy(s, q, b):
        return remote(g_tile.at[s, 2, q, half(b)], far_in.at[s, q, half(b)], gf_send.at[s, q, b], gf_recv.at[s, q, b], (iy, source))

    def part_copy(s, q, b):
        return remote(g_tile.at[s, 1, q, half(b)], part_in.at[s, q, half(b)], gp_send.at[s, q, b], gp_recv.at[s, q, b], (iy, partner))

    chunks = [(q, b) for q in (0, 1) for b in (0, 1)]

    def start_own(s):
        for q, b in chunks:
            swap_copy(s, q, b).start()

    def start_own_edges(s):
        for q, b in chunks:
            pl.when(vertical[b][1])(lambda q=q, b=b: edge_copy(s, q, b, 0).start())

    def on_swap(s, group):
        for q, b in group:
            swap_copy(s, q, b).wait_recv()
            pl.when(has_target)(lambda q=q, b=b: relay_copy(s, q, b).start())
            pl.when(vertical[b][1])(lambda q=q, b=b: edge_copy(s, q, b, 1).start())

    def on_relay(s, group):
        @pl.when(has_source)
        def _():
            for q, b in group:
                relay_copy(s, q, b).wait_recv()
                pl.when(vertical[b][1])(lambda q=q, b=b: edge_copy(s, q, b, 2).start())

    def on_edges(s):
        for q, b in chunks:
            @pl.when(vertical[1 - b][1])
            def _(q=q, b=b):
                edge_copy(s, q, b, 0).wait_recv()
                edge_copy(s, q, b, 1).wait_recv()
                pl.when(has_source)(lambda: edge_copy(s, q, b, 2).wait_recv())

    def send_rows(s):
        for t in (2, 1, 0):
            for q, b in chunks:
                pl.when(vertical[1 - b][1])(lambda q=q, b=b, t=t: rows_copy(s, q, b, t).start())

    def add_rows(s, q, b, t):
        @pl.when(vertical[b][1])
        def _():
            rows_copy(s, q, b, t).wait_recv()
            g_tile[s, t, q, half(b), :] += rows_in[s, b, t, q]

    def send_far(s):
        @pl.when(has_source)
        def _():
            for q, b in chunks:
                add_rows(s, q, b, 2)
                far_copy(s, q, b).start()

        @pl.when(jnp.logical_not(has_source))
        def _():
            for q, b in chunks:
                add_rows(s, q, b, 2)

    def send_part(s):
        for q, b in chunks:
            add_rows(s, q, b, 1)

            @pl.when(has_target)
            def _(q=q, b=b):
                far_copy(s, q, b).wait_recv()
                g_tile[s, 1, q, half(b), :] += far_in[s, q, half(b), :]

            part_copy(s, q, b).start()

    def finish(s):
        for q, b in chunks:
            add_rows(s, q, b, 0)
            part_copy(s, q, b).wait_recv()
            out_ref[s, q, half(b), :] = g_tile[s, 0, q, half(b), :] + part_in[s, q, half(b), :]

    start_own(0)
    start_own_edges(0)
    start_own(1)
    start_own_edges(1)
    loads[1].wait()
    loads[2].wait()
    tr_ref[0] = jnp.cos(phase_ref[...])
    tr_ref[1] = jnp.sin(phase_ref[...])
    for p in range(count):
        r, c = start(p)
        r = lax.rem(r, n)
        roll_ref[p, 0] = pltpu.roll(pltpu.roll(probe_ref[0], c, 1), r, 0)
        roll_ref[p, 1] = pltpu.roll(pltpu.roll(probe_ref[1], c, 1), r, 0)
    g_tile[...] = jnp.zeros_like(g_tile)
    g_edge[...] = jnp.zeros_like(g_edge)
    for load in (loads[0], *loads[3:]):
        load.wait()
    on_swap(0, chunks)
    on_relay(0, chunks)
    on_swap(1, chunks[:2])
    on_edges(0)

    def first(p, carry):
        @pl.when(p == 1)
        def _():
            on_relay(1, chunks[:2])

        mask = masks(start, p, n, odd)
        tiles = (own.at[0], part.at[0], far.at[0])
        wr = window(0, tiles, edge.at[0], mask, n)
        wi = window(1, tiles, edge.at[0], mask, n)
        xr, xi = fft2(*mul(roll_ref[p, 0], roll_ref[p, 1], wr, wi), right_ref, left_ref)
        xr, xi = mul(tr_ref[0], tr_ref[1], xr, xi)

        @pl.when(p == 0)
        def _():
            on_swap(1, chunks[2:])

        @pl.when(p == 1)
        def _():
            on_relay(1, chunks[2:])

        xr, xi = ifft2(xr, xi, right_ref, left_ref)
        phi_ref[p, 0] = xr
        phi_ref[p, 1] = xi
        return carry

    lax.fori_loop(0, count, first, 0)
    if count == 1:
        on_relay(1, chunks)
    on_edges(1)

    def second(p, carry):
        mask = masks(start, p, n, odd)
        tiles = (own.at[1], part.at[1], far.at[1])
        wr = window(0, tiles, edge.at[1], mask, n)
        wi = window(1, tiles, edge.at[1], mask, n)
        fr, fi = fft2(*mul(phi_ref[p, 0], phi_ref[p, 1], wr, wi), right_ref, left_ref)
        res = 2.0 * (fr * fr + fi * fi - intensity_ref[p])
        br, bi = ifft2(res * fr, res * fi, right_ref, left_ref)
        zr, zi = mul(wr, -wi, br, bi)
        back_ref[p, 0] = zr
        back_ref[p, 1] = zi
        gr, gi = mul(phi_ref[p, 0], -phi_ref[p, 1], br, bi)
        scatter(gr, 0, g_tile.at[1], g_edge.at[1], mask, n)
        scatter(gi, 1, g_tile.at[1], g_edge.at[1], mask, n)
        return carry

    lax.fori_loop(0, count, second, 0)
    send_rows(1)

    def third(p, carry):
        @pl.when(p == 1)
        def _():
            send_far(1)

        mask = masks(start, p, n, odd)
        xr, xi = fft2(back_ref[p, 0], back_ref[p, 1], right_ref, left_ref)
        xr, xi = ifft2(*mul(tr_ref[0], -tr_ref[1], xr, xi), right_ref, left_ref)
        gr, gi = mul(roll_ref[p, 0], -roll_ref[p, 1], xr, xi)
        scatter(gr, 0, g_tile.at[0], g_edge.at[0], mask, n)
        scatter(gi, 1, g_tile.at[0], g_edge.at[0], mask, n)
        return carry

    lax.fori_loop(0, count, third, 0)
    send_rows(0)
    if count == 1:
        send_far(1)
    send_part(1)
    send_far(0)
    send_part(0)
    finish(1)
    finish(0)
    for s in (0, 1):
        for q, b in chunks:
            swap_copy(s, q, b).wait_send()
            part_copy(s, q, b).wait_send()
            pl.when(has_target)(lambda s=s, q=q, b=b: relay_copy(s, q, b).wait_send())
            pl.when(has_source)(lambda s=s, q=q, b=b: far_copy(s, q, b).wait_send())

            @pl.when(vertical[b][1])
            def _(s=s, q=q, b=b):
                edge_copy(s, q, b, 0).wait_send()
                edge_copy(s, q, b, 1).wait_send()
                pl.when(has_source)(lambda: edge_copy(s, q, b, 2).wait_send())

            @pl.when(vertical[1 - b][1])
            def _(s=s, q=q, b=b):
                for t in (0, 1, 2):
                    rows_copy(s, q, b, t).wait_send()


def on_device(intensity, corner, probe, prop_phase, object_slices, momentum):
    count, n = intensity.shape[0], intensity.shape[-1]
    h = n // 2
    _, _, tile_rows, tile_cols = object_slices.shape
    assert tile_rows == n and tile_cols == h
    nty, ntx = lax.axis_size("ty"), lax.axis_size("tx")
    assert ntx % 2 == 0
    right, left = dft_tables(n)
    f32 = jnp.float32
    field = pltpu.VMEM((count, 2, n, n), f32)
    dma = pltpu.SemaphoreType.DMA
    tiles, edges = (2, 2, n, h), (2, 2, 3, 2, h, h)
    gradient = pl.pallas_call(
        functools.partial(kernel, (nty, ntx)),
        out_shape=jax.ShapeDtypeStruct(object_slices.shape, f32),
        in_specs=[SMEM] + [ANY] * 6,
        out_specs=VMEM,
        scratch_shapes=[
            pltpu.VMEM(object_slices.shape, f32),
            pltpu.VMEM(probe.shape, f32),
            pltpu.VMEM(prop_phase.shape, f32),
            pltpu.VMEM(right.shape, right.dtype),
            pltpu.VMEM(left.shape, left.dtype),
            pltpu.VMEM(intensity.shape, f32),
            pltpu.VMEM((2, n, n), f32),
            field,
            field,
            field,
            pltpu.VMEM(tiles, f32),
            pltpu.VMEM(tiles, f32),
            pltpu.VMEM(edges, f32),
            pltpu.VMEM((2, 3, 2, n, h), f32),
            pltpu.VMEM(edges, f32),
            pltpu.VMEM(edges, f32),
            pltpu.VMEM(tiles, f32),
            pltpu.VMEM(tiles, f32),
            dma((6,)),
        ]
        + [dma((2, 2, 2))] * 4
        + [dma((2, 2, 3, 2))] * 4
        + [dma((2, 2, 2))] * 4,
        compiler_params=pltpu.CompilerParams(
            collective_id=0, has_side_effects=True, vmem_limit_bytes=67043328
        ),
    )(corner, object_slices, probe, prop_phase, intensity, right, left)
    momentum_next = decay_rate * momentum + grad_scale * gradient
    object_next = object_slices - step_length * momentum_next
    return (object_next, momentum_next)


def solution(mesh):
    return jax.shard_map(
        on_device,
        mesh=mesh,
        in_specs=(
            P(("ty", "tx"), None, None),
            P(("ty", "tx"), None),
            P(),
            P(),
            P(None, None, "ty", "tx"),
            P(None, None, "ty", "tx"),
        ),
        out_specs=(P(None, None, "ty", "tx"), P(None, None, "ty", "tx")),
        check_vma=False,
    )
```
